32 devices in a mesh: img: 8 (over z, x), head: 4 (over y, core).
Axes of the slice: x: 2, y: 2, z: 4, core: 2. Of those that a mesh axis runs over, the one named last changes fastest.
Arguments:
- inputs: bfloat16 [2048, 1280], P('img'), may hold values from -6 to 6
- middle: bfloat16 [2048, 1280], P('img'), may hold values from -6 to 6
- out_grad: bfloat16 [2048, 1280], P('img'), may hold values from -6 to 6
- cached_maps: bfloat16 [8, 16, 256, 256], P('img', 'head'), may hold values from 0 to 1, as said below
- w_value: bfloat16 [1280, 1280], P(None, 'head'), may hold values from -0.15625 to 0.15625
- w_out: bfloat16 [1280, 1280], P('head'), may hold values from -0.15625 to 0.15625
- w_up: bfloat16 [1280, 2560], P(None, 'head'), may hold values from -0.15625 to 0.15625
- w_down: bfloat16 [2560, 1280], P('head'), may hold values from -0.125 to 0.125
Outputs:
- in_grad: bfloat16 [2048, 1280], P(('img', 'head'))
- grad_value: float32 [1280, 1280], P('img', 'head')
- grad_out: float32 [1280, 1280], P('head', 'img')
- grad_up: float32 [1280, 2560], P('img', 'head')
- grad_down: float32 [2560, 1280], P('head', 'img')
The draws below stay inside these ranges and needn't reach their ends.
Inputs may be any that keep to these rules, and one draw needn't show every extreme that they name: `cached_maps`: every row of every map is positive and sums to one up to rounding.
All inputs are finite; a program needn't handle non-finite values.
Results may differ from the reference program's by a relative error of at most 0.0069.
Values may be sent and summed in bfloat16 or wider, within the bound.
A program may use at most 128 MiB of HBM per device.

```python
import jax
import jax.numpy as jnp
from jax import lax

D = 1280
FF = 2560
HEADS = 16
TOK = 256
HDIM = 80
IMAGES = 8


def draw_cached_maps(key, part):
    first_key, second_key = jax.random.split(jax.random.fold_in(key, 7))
    sharpness = jnp.exp(jax.random.uniform(first_key, (IMAGES, HEADS, 1, 1), jnp.float32, -0.7, 1.4))
    logits = jax.random.normal(second_key, (IMAGES, HEADS, TOK, TOK), jnp.float32)
    return jax.nn.softmax(logits * sharpness, axis=-1).astype(jnp.bfloat16)


def strengthened(array, rng, source, target, parts, factor):
    owner, partner = [(jnp.arange(array.shape[axis_at]) // (array.shape[axis_at] // parts)).reshape([-1 if axis == axis_at else 1 for axis in range(array.ndim)]) for axis_at in (source, target)]
    chosen = jax.random.permutation(rng, parts)[partner]
    strong = (owner == chosen) | (owner == (partner + parts // 2) % parts)
    return jnp.where(strong, factor * array, array)


def steps_of(own_key, extent, pieces, low, top_value):
    def one(position, blocks):
        steps = jax.random.uniform(jax.random.fold_in(jax.random.fold_in(own_key, 6), position), (blocks,), jnp.float32, low / len(pieces), top_value / len(pieces))
        return jnp.repeat(jnp.exp(steps), extent[position] // blocks).reshape((-1,) + (1,) * (len(extent) - position - 1))

    level = one(*pieces[0])
    for cut in pieces[1:]:
        level = level * one(*cut)
    return level


def noise(own_key, dims, width, bound, pieces=(), kind=jnp.bfloat16):
    values = width * jax.random.normal(own_key, dims, jnp.float32)
    if pieces:
        values = values * steps_of(own_key, dims, pieces, -0.22, 0.18)
    return jnp.clip(values, -bound, bound).astype(kind)


def noise_with(stream_key, extent, scale, reach, cuts, heavy, dtype=jnp.bfloat16):
    drawn = scale * jax.random.normal(stream_key, extent, jnp.float32)
    if cuts:
        drawn = drawn * steps_of(stream_key, extent, cuts, -0.22, 0.18)
    return jnp.clip(strengthened(drawn, jax.random.fold_in(stream_key, 3), *heavy), -reach, reach).astype(dtype)


def setup_inputs(seed: int = 0) -> dict:
    key_of = jax.random.split(jax.random.key(seed), 9)
    inputs = noise_with(key_of[0], (IMAGES * TOK, D), 1.0, 6.0, ((0, 8),), (0, 1, 8, 2.0))
    middle = noise_with(key_of[1], (IMAGES * TOK, D), 1.0, 6.0, ((0, 8),), (0, 1, 8, 2.0))
    out_grad = noise_with(key_of[2], (IMAGES * TOK, D), 1.0, 6.0, ((0, 8),), (0, 1, 8, 2.0))
    cached_maps = draw_cached_maps(jax.random.fold_in(key_of[8], 71), 0)
    w_value = noise(key_of[4], (D, D), D ** -0.5, 0.15625, ((1, 4),))
    w_out = noise(key_of[5], (D, D), D ** -0.5, 0.15625, ((0, 4),))
    w_up = noise(key_of[6], (D, FF), D ** -0.5, 0.15625, ((1, 4),))
    w_down = noise(key_of[7], (FF, D), FF ** -0.5, 0.125, ((0, 4),))
    return {"inputs": inputs, "middle": middle, "out_grad": out_grad, "cached_maps": cached_maps, "w_value": w_value, "w_out": w_out, "w_up": w_up, "w_down": w_down}


def norm_rows(rows):
    centre = rows - lax.optimization_barrier(jnp.mean(rows, axis=-1, keepdims=True))
    spread = lax.optimization_barrier(jnp.mean(centre * centre, axis=-1, keepdims=True))
    return centre * lax.rsqrt(spread + 1e-06)

def norm_back(rows, grad):
    centre = rows - lax.optimization_barrier(jnp.mean(rows, axis=-1, keepdims=True))
    factor = lax.rsqrt(lax.optimization_barrier(jnp.mean(centre * centre, axis=-1, keepdims=True)) + 1e-06)
    normed = centre * factor
    return factor * (grad - lax.optimization_barrier(jnp.mean(grad, axis=-1, keepdims=True)) - normed * lax.optimization_barrier(jnp.mean(grad * normed, axis=-1, keepdims=True)))

def gelu_tanh(pre):
    return jax.nn.gelu(pre, approximate=True)

def reference(inputs, middle, out_grad, cached_maps, w_value, w_out, w_up, w_down):
    inputs_all = inputs.reshape(IMAGES, TOK, D)
    middle_all = middle.reshape(IMAGES, TOK, D)
    grads_all = out_grad.reshape(IMAGES, TOK, D)

    def one_image(totals, item):
        source, saved, upstream, maps_one = item
        source_f = source.astype(jnp.float32)
        saved_f = saved.astype(jnp.float32)
        normed_in = norm_rows(source_f).astype(jnp.bfloat16)
        values = jnp.dot(normed_in, w_value, preferred_element_type=jnp.float32).astype(jnp.bfloat16)
        maps_f = maps_one.astype(jnp.float32)
        attended = jnp.einsum('htk,khd->thd', maps_f, values.reshape(TOK, HEADS, HDIM).astype(jnp.float32))
        attended = attended.astype(jnp.bfloat16).reshape(TOK, D)
        normed_mid = norm_rows(saved_f).astype(jnp.bfloat16)
        pre = jnp.dot(normed_mid, w_up, preferred_element_type=jnp.float32)
        hidden = gelu_tanh(pre).astype(jnp.bfloat16)
        hidden_grad = jnp.dot(upstream, w_down.T, preferred_element_type=jnp.float32)
        pre_grad = jax.vjp(gelu_tanh, pre)[1](hidden_grad)[0].astype(jnp.bfloat16)
        grad_down = jnp.dot(hidden.T, upstream, preferred_element_type=jnp.float32)
        grad_up = jnp.dot(normed_mid.T, pre_grad, preferred_element_type=jnp.float32)
        mid_grad = upstream.astype(jnp.float32) + norm_back(saved_f, jnp.dot(pre_grad, w_up.T, preferred_element_type=jnp.float32))
        mid_grad_b = mid_grad.astype(jnp.bfloat16)
        grad_out = jnp.dot(attended.T, mid_grad_b, preferred_element_type=jnp.float32)
        att_grad = jnp.dot(mid_grad_b, w_out.T, preferred_element_type=jnp.float32).astype(jnp.bfloat16)
        value_grad = jnp.einsum('htk,thd->khd', maps_f, att_grad.reshape(TOK, HEADS, HDIM).astype(jnp.float32))
        value_grad = value_grad.astype(jnp.bfloat16).reshape(TOK, D)
        grad_value = jnp.dot(normed_in.T, value_grad, preferred_element_type=jnp.float32)
        in_grad = mid_grad + norm_back(source_f, jnp.dot(value_grad, w_value.T, preferred_element_type=jnp.float32))
        totals = (totals[0] + grad_value, totals[1] + grad_out, totals[2] + grad_up, totals[3] + grad_down)
        return (totals, in_grad.astype(jnp.bfloat16))
    start = (jnp.zeros((D, D), jnp.float32), jnp.zeros((D, D), jnp.float32), jnp.zeros((D, FF), jnp.float32), jnp.zeros((FF, D), jnp.float32))
    totals, in_grads = lax.scan(one_image, start, (inputs_all, middle_all, grads_all, cached_maps))
    return (in_grads.reshape(IMAGES * TOK, D), totals[0], totals[1], totals[2], totals[3])
```

```python
import jax
import jax.numpy as jnp
from jax import lax
from jax.experimental import pallas as pl
from jax.experimental.pallas import tpu as pltpu
from jax.sharding import PartitionSpec as P


def norm_rows(rows):
    centre = rows - jnp.mean(rows, axis=-1, keepdims=True)
    spread = jnp.mean(centre * centre, axis=-1, keepdims=True)
    return centre * lax.rsqrt(spread + 1e-06)


def norm_back(rows, grad):
    centre = rows - jnp.mean(rows, axis=-1, keepdims=True)
    factor = lax.rsqrt(jnp.mean(centre * centre, axis=-1, keepdims=True) + 1e-06)
    normed = centre * factor
    return factor * (
        grad
        - jnp.mean(grad, axis=-1, keepdims=True)
        - normed * jnp.mean(grad * normed, axis=-1, keepdims=True)
    )


def gelu_tanh(pre):
    return jax.nn.gelu(pre, approximate=True)


def on_device(inputs, middle, out_grad, cached_maps, w_value, w_out, w_up, w_down):
    tok_rows = inputs.shape[0]
    heads_here = cached_maps.shape[1]
    share = tok_rows // lax.axis_size("head")
    first = lax.axis_index("head") * share
    maps_here = cached_maps[0]
    normed_in = norm_rows(inputs.astype(jnp.float32)).astype(jnp.bfloat16)
    values = jnp.dot(normed_in, w_value, preferred_element_type=jnp.float32).astype(jnp.bfloat16)
    head_size = values.shape[1] // heads_here
    attended = jnp.einsum(
        "htk,khd->thd",
        maps_here,
        values.reshape(tok_rows, heads_here, head_size),
        preferred_element_type=jnp.float32,
    )
    attended = attended.astype(jnp.bfloat16).reshape(tok_rows, -1)
    middle_f = middle.astype(jnp.float32)
    normed_mid = norm_rows(middle_f).astype(jnp.bfloat16)
    pre = jnp.dot(normed_mid, w_up, preferred_element_type=jnp.float32)
    hidden = gelu_tanh(pre).astype(jnp.bfloat16)
    hidden_grad = jnp.einsum("td,fd->tf", out_grad, w_down, preferred_element_type=jnp.float32)
    pre_grad = jax.vjp(gelu_tanh, pre)[1](hidden_grad)[0].astype(jnp.bfloat16)
    down_term = jnp.einsum("tf,td->fd", hidden, out_grad, preferred_element_type=jnp.float32)
    mid_part = jnp.einsum("tf,df->td", pre_grad, w_up, preferred_element_type=jnp.float32)
    out_rows = lax.dynamic_slice_in_dim(out_grad, first, share, 0).astype(jnp.float32)
    mid_share = lax.psum_scatter(mid_part, "head", scatter_dimension=0, tiled=True)
    mid_own = out_rows + norm_back(lax.dynamic_slice_in_dim(middle_f, first, share, 0), mid_share)
    mid_grad_b = lax.all_gather(mid_own.astype(jnp.bfloat16), "head", axis=0, tiled=True)
    outproj_term = jnp.einsum("te,td->ed", attended, mid_grad_b, preferred_element_type=jnp.float32)
    att_grad = jnp.einsum(
        "td,ed->te", mid_grad_b, w_out, preferred_element_type=jnp.float32
    ).astype(jnp.bfloat16)
    value_grad = jnp.einsum(
        "htk,thd->khd",
        maps_here,
        att_grad.reshape(tok_rows, heads_here, head_size),
        preferred_element_type=jnp.float32,
    )
    value_grad = value_grad.astype(jnp.bfloat16).reshape(tok_rows, -1)
    input_part = jnp.einsum("te,de->td", value_grad, w_value, preferred_element_type=jnp.float32)
    inputs_own = lax.dynamic_slice_in_dim(inputs, first, share, 0).astype(jnp.float32)
    input_share = lax.psum_scatter(input_part, "head", scatter_dimension=0, tiled=True)
    in_grad = (mid_own + norm_back(inputs_own, input_share)).astype(jnp.bfloat16)
    picked = normed_mid
    up_term = jnp.einsum("tr,tf->rf", picked, pre_grad, preferred_element_type=jnp.float32)
    picked = normed_in
    value_term = jnp.einsum("tr,te->re", picked, value_grad, preferred_element_type=jnp.float32)
    grad_down, grad_out = (
        lax.psum_scatter(down_term, "img", scatter_dimension=1, tiled=True),
        lax.psum_scatter(outproj_term, "img", scatter_dimension=1, tiled=True),
    )
    grad_up, grad_value = (
        lax.psum_scatter(up_term, "img", scatter_dimension=0, tiled=True),
        lax.psum_scatter(value_term, "img", scatter_dimension=0, tiled=True),
    )
    return (in_grad, grad_value, grad_out, grad_up, grad_down)


MESH = pl.DeviceIdType.MESH
F32 = jnp.float32
BF16 = jnp.bfloat16
GELU_C = 0.7978845608028654


def dot_nn(a, b):
    return lax.dot_general(a, b, (((1,), (0,)), ((), ())), preferred_element_type=F32)


def dot_nt(a, b):
    return lax.dot_general(a, b, (((1,), (1,)), ((), ())), preferred_element_type=F32)


def dot_tn(a, b):
    return lax.dot_general(a, b, (((0,), (0,)), ((), ())), preferred_element_type=F32)


def gelu_and_slope(pre):
    square = pre * pre
    tanh = jnp.tanh(GELU_C * pre * (1.0 + 0.044715 * square))
    half = 0.5 * (1.0 + tanh)
    slope = half + 0.5 * pre * (1.0 - tanh * tanh) * (GELU_C * (1.0 + 3 * 0.044715 * square))
    return pre * half, slope


def block_kernel(
    inputs, middle, out_grad, maps, w_value, w_out, w_up, w_down,
    in_grad, value_rows, out_rows_t, up_rows, down_rows_t,
    mid2, og2, nm, nin, hid, prg, attd, vgr, mp, rs1, rs2, midb, mid_own,
    mlp_buf, att_buf, xr, xs, zr1, zr2, send_sem, recv_sem,
):
    tok, width = inputs.shape
    share = tok // 4
    half_rows = tok // 2
    heads_here = maps.shape[0]
    local = attd.shape[1]
    hdim = local // heads_here
    ff = hid.shape[2]
    img = lax.axis_index("img")
    head = lax.axis_index("head")
    z = img // 2
    x = img % 2
    core = head % 2
    x_peer = {"img": z * 2 + (1 - x)}
    core_peer = {"head": head + 1 - 2 * core}
    head_ids = [(head + p) % 4 for p in (1, 2, 3)]
    z_ids = [(z + q) % 4 for q in (1, 2, 3)]

    def copy(src, dst, sem, peer):
        return pltpu.make_async_remote_copy(
            src_ref=src, dst_ref=dst, send_sem=send_sem.at[sem], recv_sem=recv_sem.at[sem],
            device_id=peer, device_id_type=MESH,
        )

    barrier = pltpu.get_barrier_semaphore()
    for peer in [x_peer] + [{"head": h} for h in head_ids] + [{"img": k * 2 + x} for k in z_ids]:
        pl.semaphore_signal(barrier, inc=1, device_id=peer, device_id_type=MESH)
    pl.semaphore_wait(barrier, 7)

    mine = pl.ds(pl.multiple_of(core * half_rows, half_rows), half_rows)
    gather = [
        copy(middle.at[mine], mid2.at[mine], 0, x_peer),
        copy(out_grad.at[mine], og2.at[mine], 1, x_peer),
    ]
    for c in gather:
        c.start()
    forward = [
        copy(mid2.at[mine], mid2.at[mine], 2, core_peer),
        copy(og2.at[mine], og2.at[mine], 3, core_peer),
    ]

    def mlp(slot, rows, grad):
        normed = norm_rows(rows[...].astype(F32)).astype(BF16)
        nm[slot] = normed
        pre = dot_nn(normed, w_up[...])
        value, slope = gelu_and_slope(pre)
        hid[slot] = value.astype(BF16)
        prg[slot] = (slope * dot_nt(grad[...], w_down[...])).astype(BF16)

    mlp(0, middle, out_grad)
    mp[0] = dot_nt(prg[0], w_up[...]).astype(BF16)

    def scatter(slot, landing, first_sem):
        return [
            copy(mp.at[slot, pl.ds(pl.multiple_of(h * share, share), share)], landing.at[p], first_sem + p, {"head": h})
            for p, h in enumerate(head_ids)
        ]

    own = pl.ds(pl.multiple_of(head * share, share), share)
    scatter1 = scatter(0, rs1, 4)
    for c in scatter1:
        c.start()

    nin[...] = norm_rows(inputs[...].astype(F32)).astype(BF16)
    values = dot_nn(nin[...], w_value[...]).astype(BF16)
    column = lax.broadcasted_iota(jnp.int32, (tok, local), 1)

    def own_columns(array, h):
        keep = (column >= h * hdim) & (column < (h + 1) * hdim)
        return jnp.where(keep, array, jnp.zeros_like(array))

    total = dot_nn(maps[0], own_columns(values, 0))
    for h in range(1, heads_here):
        total = total + dot_nn(maps[h], own_columns(values, h))
    attd[...] = total.astype(BF16)

    for c in gather:
        c.wait_recv()
    for c in forward:
        c.start()

    for c in scatter1:
        c.wait_recv()
    grad_sum = mp[0, own].astype(F32) + rs1[0].astype(F32) + rs1[1].astype(F32) + rs1[2].astype(F32)
    mid_rows = out_grad[own].astype(F32) + norm_back(middle[own].astype(F32), grad_sum)
    mid_own[...] = mid_rows
    midb[own] = mid_rows.astype(BF16)
    spread = [copy(midb.at[own], midb.at[own], 7 + p, {"head": h}) for p, h in enumerate(head_ids)]
    for c in spread:
        c.start()

    for c in forward:
        c.wait_recv()
    mlp(1, mid2, og2)

    tile = 256

    def mlp_terms(step, carry):
        cols = pl.ds(pl.multiple_of(step * tile, tile), tile)
        down = dot_tn(out_grad[:, cols], hid[0]) + dot_tn(og2[:, cols], hid[1])
        up = dot_tn(nm[0, :, cols], prg[0]) + dot_tn(nm[1, :, cols], prg[1])
        mlp_buf[cols, 0:ff] = down.astype(BF16)
        mlp_buf[cols, ff:2 * ff] = up.astype(BF16)
        return carry

    lax.fori_loop(0, width // tile, mlp_terms, 0)
    piece = up_rows.shape[0]

    def chunk(at_z, at_x):
        return pl.ds(pl.multiple_of((at_z * 2 + at_x) * piece, piece), piece)

    z_mlp = [
        copy(mlp_buf.at[chunk(k, x)], zr1.at[q], 10 + q, {"img": k * 2 + x}) for q, k in enumerate(z_ids)
    ]
    for c in z_mlp:
        c.start()

    for c in spread:
        c.wait_recv()
    att_grad = dot_nt(midb[...], w_out[...]).astype(BF16)
    total = dot_tn(maps[0], own_columns(att_grad, 0))
    for h in range(1, heads_here):
        total = total + dot_tn(maps[h], own_columns(att_grad, h))
    vgr[...] = total.astype(BF16)
    mp[1] = dot_nt(vgr[...], w_value[...]).astype(BF16)
    scatter2 = scatter(1, rs2, 13)
    for c in scatter2:
        c.start()

    def att_terms(step, carry):
        cols = pl.ds(pl.multiple_of(step * tile, tile), tile)
        att_buf[cols, 0:local] = dot_tn(midb[:, cols], attd[...]).astype(BF16)
        att_buf[cols, local:2 * local] = dot_tn(nin[:, cols], vgr[...]).astype(BF16)
        return carry

    lax.fori_loop(0, width // tile, att_terms, 0)
    order = z_ids + [z]
    x_att = [copy(att_buf.at[chunk(k, 1 - x)], xr.at[q], 16 + q, x_peer) for q, k in enumerate(order)]
    for c in x_att:
        c.start()

    for c in scatter2:
        c.wait_recv()
    grad_sum = mp[1, own].astype(F32) + rs2[0].astype(F32) + rs2[1].astype(F32) + rs2[2].astype(F32)
    in_grad[...] = (mid_own[...] + norm_back(inputs[own].astype(F32), grad_sum)).astype(BF16)

    z_att = []
    for q, k in enumerate(z_ids):
        x_att[q].wait_recv()
        xs[q] = (att_buf[chunk(k, x)].astype(F32) + xr[q].astype(F32)).astype(BF16)
        c = copy(xs.at[q], zr2.at[q], 20 + q, {"img": k * 2 + x})
        c.start()
        z_att.append(c)
    x_att[3].wait_recv()

    for c in z_mlp:
        c.wait_recv()
    total = mlp_buf[chunk(z, x)].astype(F32) + zr1[0].astype(F32) + zr1[1].astype(F32) + zr1[2].astype(F32)
    down_rows_t[...] = total[:, 0:ff]
    up_rows[...] = total[:, ff:2 * ff]
    for c in z_att:
        c.wait_recv()
    total = att_buf[chunk(z, x)].astype(F32) + xr[3].astype(F32)
    total = total + zr2[0].astype(F32) + zr2[1].astype(F32) + zr2[2].astype(F32)
    out_rows_t[...] = total[:, 0:local]
    value_rows[...] = total[:, local:2 * local]
    for c in gather + forward + scatter1 + spread + z_mlp + scatter2 + x_att + z_att:
        c.wait_send()


def on_device_fused(inputs, middle, out_grad, cached_maps, w_value, w_out, w_up, w_down):
    tok, width = inputs.shape
    local, ff = w_value.shape[1], w_up.shape[1]
    piece = width // lax.axis_size("img")
    share = tok // 4
    vmem = pl.BlockSpec(memory_space=pltpu.VMEM)
    shape = jax.ShapeDtypeStruct
    in_grad, value_rows, out_rows_t, up_rows, down_rows_t = pl.pallas_call(
        block_kernel,
        out_shape=(
            shape((share, width), BF16),
            shape((piece, local), F32),
            shape((piece, local), F32),
            shape((piece, ff), F32),
            shape((piece, ff), F32),
        ),
        in_specs=[vmem] * 8,
        out_specs=(vmem,) * 5,
        scratch_shapes=[
            pltpu.VMEM((tok, width), BF16),
            pltpu.VMEM((tok, width), BF16),
            pltpu.VMEM((2, tok, width), BF16),
            pltpu.VMEM((tok, width), BF16),
            pltpu.VMEM((2, tok, ff), BF16),
            pltpu.VMEM((2, tok, ff), BF16),
            pltpu.VMEM((tok, local), BF16),
            pltpu.VMEM((tok, local), BF16),
            pltpu.VMEM((2, tok, width), BF16),
            pltpu.VMEM((3, share, width), BF16),
            pltpu.VMEM((3, share, width), BF16),
            pltpu.VMEM((tok, width), BF16),
            pltpu.VMEM((share, width), F32),
            pltpu.VMEM((width, 2 * ff), BF16),
            pltpu.VMEM((width, 2 * local), BF16),
            pltpu.VMEM((4, piece, 2 * local), BF16),
            pltpu.VMEM((3, piece, 2 * local), BF16),
            pltpu.VMEM((3, piece, 2 * ff), BF16),
            pltpu.VMEM((3, piece, 2 * local), BF16),
            pltpu.SemaphoreType.DMA((23,)),
            pltpu.SemaphoreType.DMA((23,)),
        ],
        compiler_params=pltpu.CompilerParams(
            collective_id=0, has_side_effects=True, vmem_limit_bytes=56 * 1024 * 1024
        ),
    )(inputs, middle, out_grad, cached_maps[0], w_value, w_out, w_up, w_down)
    return in_grad, value_rows, out_rows_t.T, up_rows, down_rows_t.T


def solution(mesh):
    fused = mesh.shape["img"] == 8 and mesh.shape["head"] == 4
    return jax.shard_map(
        on_device_fused if fused else on_device,
        mesh=mesh,
        in_specs=(
            P("img", None),
            P("img", None),
            P("img", None),
            P("img", "head", None, None),
            P(None, "head"),
            P("head", None),
            P(None, "head"),
            P("head", None),
        ),
        out_specs=(
            P(("img", "head"), None),
            P("img", "head"),
            P("head", "img"),
            P("img", "head"),
            P("head", "img"),
        ),
        check_vma=False,
    )
```

```python
import jax
import jax.numpy as jnp
from jax import lax
from jax.experimental import pallas as pl
from jax.experimental.pallas import tpu as pltpu
from jax.sharding import PartitionSpec as P


def norm_rows(rows):
    centre = rows - jnp.mean(rows, axis=-1, keepdims=True)
    spread = jnp.mean(centre * centre, axis=-1, keepdims=True)
    return centre * lax.rsqrt(spread + 1e-06)


def norm_back(rows, grad):
    centre = rows - jnp.mean(rows, axis=-1, keepdims=True)
    factor = lax.rsqrt(jnp.mean(centre * centre, axis=-1, keepdims=True) + 1e-06)
    normed = centre * factor
    return factor * (
        grad
        - jnp.mean(grad, axis=-1, keepdims=True)
        - normed * jnp.mean(grad * normed, axis=-1, keepdims=True)
    )


def gelu_tanh(pre):
    return jax.nn.gelu(pre, approximate=True)


def on_device(inputs, middle, out_grad, cached_maps, w_value, w_out, w_up, w_down):
    tok_rows = inputs.shape[0]
    heads_here = cached_maps.shape[1]
    share = tok_rows // lax.axis_size("head")
    first = lax.axis_index("head") * share
    maps_here = cached_maps[0]
    normed_in = norm_rows(inputs.astype(jnp.float32)).astype(jnp.bfloat16)
    values = jnp.dot(normed_in, w_value, preferred_element_type=jnp.float32).astype(jnp.bfloat16)
    head_size = values.shape[1] // heads_here
    attended = jnp.einsum(
        "htk,khd->thd",
        maps_here,
        values.reshape(tok_rows, heads_here, head_size),
        preferred_element_type=jnp.float32,
    )
    attended = attended.astype(jnp.bfloat16).reshape(tok_rows, -1)
    middle_f = middle.astype(jnp.float32)
    normed_mid = norm_rows(middle_f).astype(jnp.bfloat16)
    pre = jnp.dot(normed_mid, w_up, preferred_element_type=jnp.float32)
    hidden = gelu_tanh(pre).astype(jnp.bfloat16)
    hidden_grad = jnp.einsum("td,fd->tf", out_grad, w_down, preferred_element_type=jnp.float32)
    pre_grad = jax.vjp(gelu_tanh, pre)[1](hidden_grad)[0].astype(jnp.bfloat16)
    down_term = jnp.einsum("tf,td->fd", hidden, out_grad, preferred_element_type=jnp.float32)
    mid_part = jnp.einsum("tf,df->td", pre_grad, w_up, preferred_element_type=jnp.float32)
    out_rows = lax.dynamic_slice_in_dim(out_grad, first, share, 0).astype(jnp.float32)
    mid_share = lax.psum_scatter(mid_part, "head", scatter_dimension=0, tiled=True)
    mid_own = out_rows + norm_back(lax.dynamic_slice_in_dim(middle_f, first, share, 0), mid_share)
    mid_grad_b = lax.all_gather(mid_own.astype(jnp.bfloat16), "head", axis=0, tiled=True)
    outproj_term = jnp.einsum("te,td->ed", attended, mid_grad_b, preferred_element_type=jnp.float32)
    att_grad = jnp.einsum(
        "td,ed->te", mid_grad_b, w_out, preferred_element_type=jnp.float32
    ).astype(jnp.bfloat16)
    value_grad = jnp.einsum(
        "htk,thd->khd",
        maps_here,
        att_grad.reshape(tok_rows, heads_here, head_size),
        preferred_element_type=jnp.float32,
    )
    value_grad = value_grad.astype(jnp.bfloat16).reshape(tok_rows, -1)
    input_part = jnp.einsum("te,de->td", value_grad, w_value, preferred_element_type=jnp.float32)
    inputs_own = lax.dynamic_slice_in_dim(inputs, first, share, 0).astype(jnp.float32)
    input_share = lax.psum_scatter(input_part, "head", scatter_dimension=0, tiled=True)
    in_grad = (mid_own + norm_back(inputs_own, input_share)).astype(jnp.bfloat16)
    picked = normed_mid
    up_term = jnp.einsum("tr,tf->rf", picked, pre_grad, preferred_element_type=jnp.float32)
    picked = normed_in
    value_term = jnp.einsum("tr,te->re", picked, value_grad, preferred_element_type=jnp.float32)
    grad_down, grad_out = (
        lax.psum_scatter(down_term, "img", scatter_dimension=1, tiled=True),
        lax.psum_scatter(outproj_term, "img", scatter_dimension=1, tiled=True),
    )
    grad_up, grad_value = (
        lax.psum_scatter(up_term, "img", scatter_dimension=0, tiled=True),
        lax.psum_scatter(value_term, "img", scatter_dimension=0, tiled=True),
    )
    return (in_grad, grad_value, grad_out, grad_up, grad_down)


MESH = pl.DeviceIdType.MESH
F32 = jnp.float32
BF16 = jnp.bfloat16
GELU_C = 0.7978845608028654


def dot_nn(a, b):
    return lax.dot_general(a, b, (((1,), (0,)), ((), ())), preferred_element_type=F32)


def dot_nt(a, b):
    return lax.dot_general(a, b, (((1,), (1,)), ((), ())), preferred_element_type=F32)


def dot_tn(a, b):
    return lax.dot_general(a, b, (((0,), (0,)), ((), ())), preferred_element_type=F32)


def gelu_and_slope(pre):
    square = pre * pre
    tanh = jnp.tanh(GELU_C * pre * (1.0 + 0.044715 * square))
    half = 0.5 * (1.0 + tanh)
    slope = half + 0.5 * pre * (1.0 - tanh * tanh) * (GELU_C * (1.0 + 3 * 0.044715 * square))
    return pre * half, slope


def block_kernel(
    inputs_h, middle_h, out_grad_h, maps_h, w_value_h, w_out_h, w_up_h, w_down_h,
    in_grad, mlp_sum, att_sum,
    inputs, middle, out_grad, maps, w_value_t, w_out, w_up, w_down,
    mid2, og2, nmt, ogt, nint, midbt, hid, prg, attd, vgr, mp, rs1, rs2, midb, mid_own,
    mlp_buf, att_buf, xr, zr1, zs1, zr2, zs2, local_sem, send_sem, recv_sem,
):
    tok, width = inputs.shape
    share = tok // 4
    quarter = tok // 4
    heads_here = maps.shape[0]
    local = attd.shape[1]
    hdim = local // heads_here
    ff = hid.shape[2]
    piece = mlp_sum.shape[0]
    img = lax.axis_index("img")
    head = lax.axis_index("head")
    z = img // 2
    x = img % 2
    core = head % 2
    upper = z // 2
    depth = z % 2 * (1 - 2 * upper) + upper
    x_peer = {"img": z * 2 + (1 - x)}
    core_peer = {"head": head + 1 - 2 * core}
    side_peer = {"img": (z + 1 - 2 * (z % 2)) * 2 + x}
    across_peer = {"img": (3 - z) * 2 + x}
    head_ids = [(head + p) % 4 for p in (1, 2, 3)]

    def copy(src, dst, sem, peer):
        return pltpu.make_async_remote_copy(
            src_ref=src, dst_ref=dst, send_sem=send_sem.at[sem], recv_sem=recv_sem.at[sem],
            device_id=peer, device_id_type=MESH,
        )

    barrier = pltpu.get_barrier_semaphore()
    for peer in [x_peer, side_peer, across_peer] + [{"head": h} for h in head_ids]:
        pl.semaphore_signal(barrier, inc=1, device_id=peer, device_id_type=MESH)
    loads = [
        pltpu.make_async_copy(src, dst, local_sem.at[i])
        for i, (src, dst) in enumerate([
            (middle_h, middle), (w_up_h, w_up), (out_grad_h, out_grad), (w_down_h, w_down),
            (inputs_h, inputs), (w_value_h, w_value_t), (maps_h, maps), (w_out_h, w_out),
        ])
    ]
    for c in loads:
        c.start()
    pl.semaphore_wait(barrier, 6)

    gather, forward = [], []
    for part in range(2):
        rows = pl.ds(pl.multiple_of((core * 2 + part) * quarter, quarter), quarter)
        for i, (src, dst) in enumerate([(middle_h, mid2), (out_grad_h, og2)]):
            gather.append(copy(src.at[rows], dst.at[rows], part * 2 + i, x_peer))
            forward.append(copy(dst.at[rows], dst.at[rows], 4 + part * 2 + i, core_peer))
    for c in gather:
        c.start()

    def mlp(slot, rows, grad):
        normed = norm_rows(rows[...].astype(F32)).astype(BF16)
        nmt[slot] = normed.T
        pre = dot_nn(normed, w_up[...])
        value, slope = gelu_and_slope(pre)
        hid[slot] = value.astype(BF16)
        prg[slot] = (slope * dot_nt(grad[...], w_down[...])).astype(BF16)

    for c in loads[:4]:
        c.wait()
    mlp(0, middle, out_grad)
    mp[0] = dot_nt(prg[0], w_up[...]).astype(BF16)

    def scatter(slot, landing, first_sem):
        return [
            copy(mp.at[slot, pl.ds(pl.multiple_of(h * share, share), share)], landing.at[p], first_sem + p, {"head": h})
            for p, h in enumerate(head_ids)
        ]

    own = pl.ds(pl.multiple_of(head * share, share), share)
    scatter1 = scatter(0, rs1, 8)
    for c in scatter1:
        c.start()

    for c in loads[4:]:
        c.wait()
    ogt[0] = out_grad[...].T
    normed_in = norm_rows(inputs[...].astype(F32)).astype(BF16)
    nint[...] = normed_in.T
    values = dot_nt(normed_in, w_value_t[...]).astype(BF16)
    column = lax.broadcasted_iota(jnp.int32, (tok, local), 1)

    def own_columns(array, h):
        keep = (column >= h * hdim) & (column < (h + 1) * hdim)
        return jnp.where(keep, array, jnp.zeros_like(array))

    total = dot_nn(maps[0], own_columns(values, 0))
    for h in range(1, heads_here):
        total = total + dot_nn(maps[h], own_columns(values, h))
    attd[...] = total.astype(BF16)

    for got, c in zip(gather, forward):
        got.wait_recv()
        c.start()

    for c in scatter1:
        c.wait_recv()
    grad_sum = mp[0, own].astype(F32) + rs1[0].astype(F32) + rs1[1].astype(F32) + rs1[2].astype(F32)
    mid_rows = out_grad[own].astype(F32) + norm_back(middle[own].astype(F32), grad_sum)
    mid_own[...] = mid_rows
    midb[own] = mid_rows.astype(BF16)
    spread = [copy(midb.at[own], midb.at[own], 11 + p, {"head": h}) for p, h in enumerate(head_ids)]
    for c in spread:
        c.start()

    for c in forward:
        c.wait_recv()
    mlp(1, mid2, og2)
    ogt[1] = og2[...].T

    def actual(c):
        return c * (1 - 2 * upper) + 3 * upper

    def chunk(c, at_x):
        return pl.ds(pl.multiple_of((actual(c) * 2 + at_x) * piece, piece), piece)

    def exchange(buf, zr, zs, first_sem):
        ends = [copy(buf.at[c], zr.at[i], first_sem + i, side_peer) for i, c in enumerate((3, 2, 1))]
        cross = [copy(zs.at[i], zr.at[3 + i], first_sem + 3 + i, across_peer) for i in range(2)]
        back = copy(zs.at[2], zr.at[5], first_sem + 5, side_peer)
        return ends, cross, back

    ends1, cross1, back1 = exchange(mlp_buf, zr1, zs1, 14)
    ends2, cross2, back2 = exchange(att_buf, zr2, zs2, 20)

    for i, c in enumerate((3, 2, 1, 0)):
        rows = chunk(c, x)
        down = dot_nn(ogt[0, rows], hid[0]) + dot_nn(ogt[1, rows], hid[1])
        up = dot_nn(nmt[0, rows], prg[0]) + dot_nn(nmt[1, rows], prg[1])
        mlp_buf[c, :, 0:ff] = down.astype(BF16)
        mlp_buf[c, :, ff:2 * ff] = up.astype(BF16)
        if i < 3:
            @pl.when(depth == 0)
            def _():
                ends1[i].start()

    for c in spread:
        c.wait_recv()
    att_grad = dot_nt(midb[...], w_out[...]).astype(BF16)
    total = dot_tn(maps[0], own_columns(att_grad, 0))
    for h in range(1, heads_here):
        total = total + dot_tn(maps[h], own_columns(att_grad, h))
    vgr[...] = total.astype(BF16)
    mp[1] = dot_nn(vgr[...], w_value_t[...]).astype(BF16)
    scatter2 = scatter(1, rs2, 26)
    for c in scatter2:
        c.start()
    midbt[...] = midb[...].T

    x_att = []
    for to_peer in (True, False):
        for i, c in enumerate((3, 2, 1, 0)):
            rows = chunk(c, 1 - x if to_peer else x)
            slot = 4 + c if to_peer else c
            att_buf[slot, :, 0:local] = dot_nn(midbt[rows], attd[...]).astype(BF16)
            att_buf[slot, :, local:2 * local] = dot_nn(nint[rows], vgr[...]).astype(BF16)
            if to_peer:
                x_att.append(copy(att_buf.at[slot], xr.at[c], 29 + c, x_peer))
                x_att[i].start()

    def add(buf, zs, zr, slot, c, i):
        zs[slot] = (buf[c].astype(F32) + zr[i].astype(F32)).astype(BF16)

    @pl.when(depth == 1)
    def _():
        ends1[0].wait_recv()
        add(mlp_buf, zs1, zr1, 0, 3, 0)
        cross1[0].start()

    for c in scatter2:
        c.wait_recv()
    grad_sum = mp[1, own].astype(F32) + rs2[0].astype(F32) + rs2[1].astype(F32) + rs2[2].astype(F32)
    in_grad[...] = (mid_own[...] + norm_back(inputs[own].astype(F32), grad_sum)).astype(BF16)

    @pl.when(depth == 1)
    def _():
        ends1[1].wait_recv()
        add(mlp_buf, zs1, zr1, 1, 2, 1)
        cross1[1].start()
        cross1[0].wait_recv()
        add(mlp_buf, zs1, zr1, 2, 0, 3)
        back1.start()

    for i, c in enumerate((3, 2, 1, 0)):
        x_att[i].wait_recv()
        att_buf[c] = (att_buf[c].astype(F32) + xr[c].astype(F32)).astype(BF16)
        if i < 3:
            @pl.when(depth == 0)
            def _():
                ends2[i].start()

    @pl.when(depth == 1)
    def _():
        ends2[0].wait_recv()
        add(att_buf, zs2, zr2, 0, 3, 0)
        cross2[0].start()
        ends2[1].wait_recv()
        add(att_buf, zs2, zr2, 1, 2, 1)
        cross2[1].start()
        cross2[0].wait_recv()
        add(att_buf, zs2, zr2, 2, 0, 3)
        back2.start()
        for ends, cross, back, buf, zr, result in (
            (ends1, cross1, back1, mlp_buf, zr1, mlp_sum),
            (ends2, cross2, back2, att_buf, zr2, att_sum),
        ):
            ends[2].wait_recv()
            cross[1].wait_recv()
            result[...] = buf[1].astype(F32) + zr[2].astype(F32) + zr[4].astype(F32)
            for c in cross + [back]:
                c.wait_send()

    @pl.when(depth == 0)
    def _():
        for ends, back, buf, zr, result in (
            (ends1, back1, mlp_buf, zr1, mlp_sum),
            (ends2, back2, att_buf, zr2, att_sum),
        ):
            back.wait_recv()
            result[...] = buf[0].astype(F32) + zr[5].astype(F32)
            for c in ends:
                c.wait_send()

    for c in gather + forward + scatter1 + spread + scatter2 + x_att:
        c.wait_send()


def split_kernel(in_grad, mlp_sum, att_sum, in_grad_out, value_rows, out_rows_t, up_rows, down_rows_t):
    local, ff = value_rows.shape[1], up_rows.shape[1]
    in_grad_out[...] = in_grad[...]
    down_rows_t[...] = mlp_sum[:, 0:ff]
    up_rows[...] = mlp_sum[:, ff:2 * ff]
    out_rows_t[...] = att_sum[:, 0:local]
    value_rows[...] = att_sum[:, local:2 * local]


def on_device_fused(inputs, middle, out_grad, cached_maps, w_value, w_out, w_up, w_down):
    tok, width = inputs.shape
    local, ff = w_value.shape[1], w_up.shape[1]
    heads_here = cached_maps.shape[1]
    piece = width // lax.axis_size("img")
    share = tok // 4
    vmem = pl.BlockSpec(memory_space=pltpu.VMEM)
    shape = jax.ShapeDtypeStruct
    sums = pl.pallas_call(
        block_kernel,
        out_shape=(
            shape((share, width), BF16),
            shape((piece, 2 * ff), F32),
            shape((piece, 2 * local), F32),
        ),
        in_specs=[pl.BlockSpec(memory_space=pl.ANY)] * 8,
        out_specs=(vmem,) * 3,
        scratch_shapes=[
            pltpu.VMEM((tok, width), BF16),
            pltpu.VMEM((tok, width), BF16),
            pltpu.VMEM((tok, width), BF16),
            pltpu.VMEM((heads_here, tok, tok), BF16),
            pltpu.VMEM((local, width), BF16),
            pltpu.VMEM((local, width), BF16),
            pltpu.VMEM((width, ff), BF16),
            pltpu.VMEM((ff, width), BF16),
            pltpu.VMEM((tok, width), BF16),
            pltpu.VMEM((tok, width), BF16),
            pltpu.VMEM((2, width, tok), BF16),
            pltpu.VMEM((2, width, tok), BF16),
            pltpu.VMEM((width, tok), BF16),
            pltpu.VMEM((width, tok), BF16),
            pltpu.VMEM((2, tok, ff), BF16),
            pltpu.VMEM((2, tok, ff), BF16),
            pltpu.VMEM((tok, local), BF16),
            pltpu.VMEM((tok, local), BF16),
            pltpu.VMEM((2, tok, width), BF16),
            pltpu.VMEM((3, share, width), BF16),
            pltpu.VMEM((3, share, width), BF16),
            pltpu.VMEM((tok, width), BF16),
            pltpu.VMEM((share, width), F32),
            pltpu.VMEM((4, piece, 2 * ff), BF16),
            pltpu.VMEM((8, piece, 2 * local), BF16),
            pltpu.VMEM((4, piece, 2 * local), BF16),
            pltpu.VMEM((6, piece, 2 * ff), BF16),
            pltpu.VMEM((3, piece, 2 * ff), BF16),
            pltpu.VMEM((6, piece, 2 * local), BF16),
            pltpu.VMEM((3, piece, 2 * local), BF16),
            pltpu.SemaphoreType.DMA((8,)),
            pltpu.SemaphoreType.DMA((33,)),
            pltpu.SemaphoreType.DMA((33,)),
        ],
        compiler_params=pltpu.CompilerParams(
            collective_id=0, has_side_effects=True, vmem_limit_bytes=56 * 1024 * 1024
        ),
    )(inputs, middle, out_grad, cached_maps[0], w_value.T, w_out, w_up, w_down)
    in_grad, value_rows, out_rows_t, up_rows, down_rows_t = pl.pallas_call(
        split_kernel,
        out_shape=(
            shape((share, width), BF16),
            shape((piece, local), F32),
            shape((piece, local), F32),
            shape((piece, ff), F32),
            shape((piece, ff), F32),
        ),
        in_specs=[vmem] * 3,
        out_specs=(vmem,) * 5,
    )(*sums)
    return in_grad, value_rows, out_rows_t.T, up_rows, down_rows_t.T


def solution(mesh):
    fused = mesh.shape["img"] == 8 and mesh.shape["head"] == 4
    return jax.shard_map(
        on_device_fused if fused else on_device,
        mesh=mesh,
        in_specs=(
            P("img", None),
            P("img", None),
            P("img", None),
            P("img", "head", None, None),
            P(None, "head"),
            P("head", None),
            P(None, "head"),
            P("head", None),
        ),
        out_specs=(
            P(("img", "head"), None),
            P("img", "head"),
            P("head", "img"),
            P("img", "head"),
            P("head", "img"),
        ),
        check_vma=False,
    )
```

```python
import jax
import jax.numpy as jnp
from jax import lax
from jax.experimental import pallas as pl
from jax.experimental.pallas import tpu as pltpu
from jax.sharding import PartitionSpec as P


def norm_rows(rows):
    centre = rows - jnp.mean(rows, axis=-1, keepdims=True)
    spread = jnp.mean(centre * centre, axis=-1, keepdims=True)
    return centre * lax.rsqrt(spread + 1e-06)


def norm_back(rows, grad):
    centre = rows - jnp.mean(rows, axis=-1, keepdims=True)
    factor = lax.rsqrt(jnp.mean(centre * centre, axis=-1, keepdims=True) + 1e-06)
    normed = centre * factor
    return factor * (
        grad
        - jnp.mean(grad, axis=-1, keepdims=True)
        - normed * jnp.mean(grad * normed, axis=-1, keepdims=True)
    )


def gelu_tanh(pre):
    return jax.nn.gelu(pre, approximate=True)


def on_device(inputs, middle, out_grad, cached_maps, w_value, w_out, w_up, w_down):
    tok_rows = inputs.shape[0]
    heads_here = cached_maps.shape[1]
    share = tok_rows // lax.axis_size("head")
    first = lax.axis_index("head") * share
    maps_here = cached_maps[0]
    normed_in = norm_rows(inputs.astype(jnp.float32)).astype(jnp.bfloat16)
    values = jnp.dot(normed_in, w_value, preferred_element_type=jnp.float32).astype(jnp.bfloat16)
    head_size = values.shape[1] // heads_here
    attended = jnp.einsum(
        "htk,khd->thd",
        maps_here,
        values.reshape(tok_rows, heads_here, head_size),
        preferred_element_type=jnp.float32,
    )
    attended = attended.astype(jnp.bfloat16).reshape(tok_rows, -1)
    middle_f = middle.astype(jnp.float32)
    normed_mid = norm_rows(middle_f).astype(jnp.bfloat16)
    pre = jnp.dot(normed_mid, w_up, preferred_element_type=jnp.float32)
    hidden = gelu_tanh(pre).astype(jnp.bfloat16)
    hidden_grad = jnp.einsum("td,fd->tf", out_grad, w_down, preferred_element_type=jnp.float32)
    pre_grad = jax.vjp(gelu_tanh, pre)[1](hidden_grad)[0].astype(jnp.bfloat16)
    down_term = jnp.einsum("tf,td->fd", hidden, out_grad, preferred_element_type=jnp.float32)
    mid_part = jnp.einsum("tf,df->td", pre_grad, w_up, preferred_element_type=jnp.float32)
    out_rows = lax.dynamic_slice_in_dim(out_grad, first, share, 0).astype(jnp.float32)
    mid_share = lax.psum_scatter(mid_part, "head", scatter_dimension=0, tiled=True)
    mid_own = out_rows + norm_back(lax.dynamic_slice_in_dim(middle_f, first, share, 0), mid_share)
    mid_grad_b = lax.all_gather(mid_own.astype(jnp.bfloat16), "head", axis=0, tiled=True)
    outproj_term = jnp.einsum("te,td->ed", attended, mid_grad_b, preferred_element_type=jnp.float32)
    att_grad = jnp.einsum(
        "td,ed->te", mid_grad_b, w_out, preferred_element_type=jnp.float32
    ).astype(jnp.bfloat16)
    value_grad = jnp.einsum(
        "htk,thd->khd",
        maps_here,
        att_grad.reshape(tok_rows, heads_here, head_size),
        preferred_element_type=jnp.float32,
    )
    value_grad = value_grad.astype(jnp.bfloat16).reshape(tok_rows, -1)
    input_part = jnp.einsum("te,de->td", value_grad, w_value, preferred_element_type=jnp.float32)
    inputs_own = lax.dynamic_slice_in_dim(inputs, first, share, 0).astype(jnp.float32)
    input_share = lax.psum_scatter(input_part, "head", scatter_dimension=0, tiled=True)
    in_grad = (mid_own + norm_back(inputs_own, input_share)).astype(jnp.bfloat16)
    picked = normed_mid
    up_term = jnp.einsum("tr,tf->rf", picked, pre_grad, preferred_element_type=jnp.float32)
    picked = normed_in
    value_term = jnp.einsum("tr,te->re", picked, value_grad, preferred_element_type=jnp.float32)
    grad_down, grad_out = (
        lax.psum_scatter(down_term, "img", scatter_dimension=1, tiled=True),
        lax.psum_scatter(outproj_term, "img", scatter_dimension=1, tiled=True),
    )
    grad_up, grad_value = (
        lax.psum_scatter(up_term, "img", scatter_dimension=0, tiled=True),
        lax.psum_scatter(value_term, "img", scatter_dimension=0, tiled=True),
    )
    return (in_grad, grad_value, grad_out, grad_up, grad_down)


MESH = pl.DeviceIdType.MESH
F32 = jnp.float32
BF16 = jnp.bfloat16
EARLY = 128
GELU_C = 0.7978845608028654


def dot_nn(a, b):
    return lax.dot_general(a, b, (((1,), (0,)), ((), ())), preferred_element_type=F32)


def dot_nt(a, b):
    return lax.dot_general(a, b, (((1,), (1,)), ((), ())), preferred_element_type=F32)


def dot_tn(a, b):
    return lax.dot_general(a, b, (((0,), (0,)), ((), ())), preferred_element_type=F32)


def gelu_and_slope(pre):
    square = pre * pre
    tanh = jnp.tanh(GELU_C * pre * (1.0 + 0.044715 * square))
    half = 0.5 * (1.0 + tanh)
    slope = half + 0.5 * pre * (1.0 - tanh * tanh) * (GELU_C * (1.0 + 3 * 0.044715 * square))
    return pre * half, slope


def block_kernel(
    inputs_h, middle_h, out_grad_h, maps_h, w_value_h, w_out_h, w_up_h, w_down_h,
    in_grad, mlp_sum, att_sum,
    inputs, middle, out_grad, maps, w_value_t, w_out, w_up, w_down,
    nmt, ogt, nint, midbt, hid, prg, attd, vgr, mp, rs1, rs2, midb, mid_own,
    a_buf, b_buf, att_buf, xr_a, xr_b, xr, zr_a, zs_a, zr_b, zs_b, zr2, zs2, xs_a,
    local_sem, send_sem, recv_sem,
):
    tok, width = inputs.shape
    share = tok // 4
    heads_here = maps.shape[0]
    local = attd.shape[1]
    hdim = local // heads_here
    ff = hid.shape[1]
    early = a_buf.shape[2] // 2
    late = ff - early
    piece = mlp_sum.shape[0]
    img = lax.axis_index("img")
    head = lax.axis_index("head")
    z = img // 2
    x = img % 2
    upper = z // 2
    depth = z % 2 * (1 - 2 * upper) + upper
    x_peer = {"img": z * 2 + (1 - x)}
    side_peer = {"img": (z + 1 - 2 * (z % 2)) * 2 + x}
    across_peer = {"img": (3 - z) * 2 + x}
    head_ids = [(head + p) % 4 for p in (1, 2, 3)]

    def copy(src, dst, sem, peer):
        return pltpu.make_async_remote_copy(
            src_ref=src, dst_ref=dst, send_sem=send_sem.at[sem], recv_sem=recv_sem.at[sem],
            device_id=peer, device_id_type=MESH,
        )

    barrier = pltpu.get_barrier_semaphore()
    for peer in [x_peer, side_peer, across_peer] + [{"head": h} for h in head_ids]:
        pl.semaphore_signal(barrier, inc=1, device_id=peer, device_id_type=MESH)
    loads = [
        pltpu.make_async_copy(src, dst, local_sem.at[i])
        for i, (src, dst) in enumerate([
            (middle_h, middle), (w_up_h, w_up), (out_grad_h, out_grad), (w_down_h, w_down),
            (inputs_h, inputs), (w_value_h, w_value_t), (maps_h, maps), (w_out_h, w_out),
        ])
    ]
    for c in loads:
        c.start()
    pl.semaphore_wait(barrier, 6)

    for c in loads[:4]:
        c.wait()
    normed = norm_rows(middle[...].astype(F32)).astype(BF16)
    pre = dot_nn(normed, w_up[...])
    value, slope = gelu_and_slope(pre)
    hid[...] = value.astype(BF16)
    prg[...] = (slope * dot_nt(out_grad[...], w_down[...])).astype(BF16)
    mp[0] = dot_nt(prg[...], w_up[...]).astype(BF16)

    def scatter(slot, landing, first_sem):
        return [
            copy(mp.at[slot, pl.ds(pl.multiple_of(h * share, share), share)], landing.at[p], first_sem + p, {"head": h})
            for p, h in enumerate(head_ids)
        ]

    own = pl.ds(pl.multiple_of(head * share, share), share)
    scatter1 = scatter(0, rs1, 0)
    for c in scatter1:
        c.start()
    nmt[...] = normed.T
    ogt[...] = out_grad[...].T

    def actual(c):
        return c * (1 - 2 * upper) + 3 * upper

    def chunk(c, at_x):
        return pl.ds(pl.multiple_of((actual(c) * 2 + at_x) * piece, piece), piece)

    def exchange(buf, zr, zs, first_sem):
        ends = [copy(buf.at[c], zr.at[i], first_sem + i, side_peer) for i, c in enumerate((3, 2, 1))]
        cross = [copy(zs.at[i], zr.at[3 + i], first_sem + 3 + i, across_peer) for i in range(2)]
        back = copy(zs.at[2], zr.at[5], first_sem + 5, side_peer)
        return ends, cross, back

    ends_a, cross_a, back_a = exchange(a_buf, zr_a, zs_a, 18)
    ends_b, cross_b, back_b = exchange(b_buf, zr_b, zs_b, 24)
    ends2, cross2, back2 = exchange(att_buf, zr2, zs2, 30)

    def at_end(start):
        @pl.when(depth == 0)
        def _():
            start()

    def add(buf, zs, zr, slot, c, i):
        zs[slot] = (buf[c].astype(F32) + zr[i].astype(F32)).astype(BF16)

    order = (3, 2, 1 - depth, depth)
    x_b = []
    for i, c in enumerate(order):
        rows = chunk(c, 1 - x)
        b_buf[4 + c, :, 0:late] = dot_nn(ogt[rows], hid[:, early:ff]).astype(BF16)
        b_buf[4 + c, :, late:2 * late] = dot_nn(nmt[rows], prg[:, early:ff]).astype(BF16)
        x_b.append(copy(b_buf.at[4 + c], xr_b.at[i], 9 + i, x_peer))
        x_b[i].start()
        c = 3 - i
        rows = pl.ds(pl.multiple_of(actual(c) * 2 * piece, piece), 2 * piece)
        a_buf[c, :, 0:early] = dot_nn(ogt[rows], hid[:, 0:early]).astype(BF16)
        a_buf[c, :, early:2 * early] = dot_nn(nmt[rows], prg[:, 0:early]).astype(BF16)
        if i < 3:
            at_end(ends_a[i].start)
    for c in (3, 2, 1, 0):
        rows = chunk(c, x)
        b_buf[c, :, 0:late] = dot_nn(ogt[rows], hid[:, early:ff]).astype(BF16)
        b_buf[c, :, late:2 * late] = dot_nn(nmt[rows], prg[:, early:ff]).astype(BF16)

    for c in loads[4:]:
        c.wait()
    normed_in = norm_rows(inputs[...].astype(F32)).astype(BF16)
    nint[...] = normed_in.T
    values = dot_nt(normed_in, w_value_t[...]).astype(BF16)
    column = lax.broadcasted_iota(jnp.int32, (tok, local), 1)

    def own_columns(array, h):
        keep = (column >= h * hdim) & (column < (h + 1) * hdim)
        return jnp.where(keep, array, jnp.zeros_like(array))

    total = dot_nn(maps[0], own_columns(values, 0))
    for h in range(1, heads_here):
        total = total + dot_nn(maps[h], own_columns(values, h))
    attd[...] = total.astype(BF16)

    def pass_on(buf, zr, zs, ends, cross, i):
        ends[i].wait_recv()
        add(buf, zs, zr, i, 3 - i, i)
        cross[i].start()

    def give_back(buf, zr, zs, cross, back):
        cross[0].wait_recv()
        add(buf, zs, zr, 2, 0, 3)
        back.start()

    @pl.when(depth == 1)
    def _():
        pass_on(a_buf, zr_a, zs_a, ends_a, cross_a, 0)

    for c in scatter1:
        c.wait_recv()
    grad_sum = mp[0, own].astype(F32) + rs1[0].astype(F32) + rs1[1].astype(F32) + rs1[2].astype(F32)
    mid_rows = out_grad[own].astype(F32) + norm_back(middle[own].astype(F32), grad_sum)
    mid_own[...] = mid_rows
    midb[own] = mid_rows.astype(BF16)
    spread = [copy(midb.at[own], midb.at[own], 3 + p, {"head": h}) for p, h in enumerate(head_ids)]
    for c in spread:
        c.start()

    def settle_b(i):
        c = order[i]
        x_b[i].wait_recv()
        b_buf[c] = (b_buf[c].astype(F32) + xr_b[i].astype(F32)).astype(BF16)
        if i < 3:
            at_end(ends_b[i].start)

    settle_b(0)

    @pl.when(depth == 1)
    def _():
        pass_on(a_buf, zr_a, zs_a, ends_a, cross_a, 1)
        give_back(a_buf, zr_a, zs_a, cross_a, back_a)

    x_a = copy(xs_a.at[1 - x], xr_a, 13, x_peer)

    def split_a(total):
        xs_a[0] = total[0:piece].astype(BF16)
        xs_a[1] = total[piece:2 * piece].astype(BF16)

    @pl.when(depth == 1)
    def _():
        ends_a[2].wait_recv()
        cross_a[1].wait_recv()
        split_a(a_buf[1].astype(F32) + zr_a[2].astype(F32) + zr_a[4].astype(F32))
        x_a.start()

    @pl.when(depth == 0)
    def _():
        back_a.wait_recv()
        split_a(a_buf[0].astype(F32) + zr_a[5].astype(F32))
        x_a.start()

    settle_b(1)

    @pl.when(depth == 1)
    def _():
        pass_on(b_buf, zr_b, zs_b, ends_b, cross_b, 0)

    for c in spread:
        c.wait_recv()
    att_grad = dot_nt(midb[...], w_out[...]).astype(BF16)
    total = dot_tn(maps[0], own_columns(att_grad, 0))
    for h in range(1, heads_here):
        total = total + dot_tn(maps[h], own_columns(att_grad, h))
    vgr[...] = total.astype(BF16)
    midbt[...] = midb[...].T

    x_att = []
    for i, c in enumerate(order):
        rows = chunk(c, 1 - x)
        att_buf[4 + c, :, 0:local] = dot_nn(midbt[rows], attd[...]).astype(BF16)
        att_buf[4 + c, :, local:2 * local] = dot_nn(nint[rows], vgr[...]).astype(BF16)
        x_att.append(copy(att_buf.at[4 + c], xr.at[i], 14 + i, x_peer))
        x_att[i].start()
    mp[1] = dot_nn(vgr[...], w_value_t[...]).astype(BF16)
    scatter2 = scatter(1, rs2, 6)
    for c in scatter2:
        c.start()
    settle_b(2)

    @pl.when(depth == 1)
    def _():
        pass_on(b_buf, zr_b, zs_b, ends_b, cross_b, 1)
        give_back(b_buf, zr_b, zs_b, cross_b, back_b)

    for c in (3, 2, 1, 0):
        rows = chunk(c, x)
        att_buf[c, :, 0:local] = dot_nn(midbt[rows], attd[...]).astype(BF16)
        att_buf[c, :, local:2 * local] = dot_nn(nint[rows], vgr[...]).astype(BF16)

    settle_b(3)

    def settle_att(i):
        c = order[i]
        x_att[i].wait_recv()
        att_buf[c] = (att_buf[c].astype(F32) + xr[i].astype(F32)).astype(BF16)
        if i < 3:
            at_end(ends2[i].start)

    settle_att(0)
    for c in scatter2:
        c.wait_recv()
    grad_sum = mp[1, own].astype(F32) + rs2[0].astype(F32) + rs2[1].astype(F32) + rs2[2].astype(F32)
    in_grad[...] = (mid_own[...] + norm_back(inputs[own].astype(F32), grad_sum)).astype(BF16)
    x_a.wait_recv()
    total = xs_a[x].astype(F32) + xr_a[...].astype(F32)
    mlp_sum[:, 0:early] = total[:, 0:early]
    mlp_sum[:, ff:ff + early] = total[:, early:2 * early]
    settle_att(1)

    @pl.when(depth == 1)
    def _():
        pass_on(att_buf, zr2, zs2, ends2, cross2, 0)

    settle_att(2)

    @pl.when(depth == 1)
    def _():
        pass_on(att_buf, zr2, zs2, ends2, cross2, 1)
        give_back(att_buf, zr2, zs2, cross2, back2)

    settle_att(3)

    def put_b(total):
        mlp_sum[:, early:ff] = total[:, 0:late]
        mlp_sum[:, ff + early:2 * ff] = total[:, late:2 * late]

    @pl.when(depth == 1)
    def _():
        ends_b[2].wait_recv()
        cross_b[1].wait_recv()
        put_b(b_buf[1].astype(F32) + zr_b[2].astype(F32) + zr_b[4].astype(F32))
        ends2[2].wait_recv()
        cross2[1].wait_recv()
        att_sum[...] = att_buf[1].astype(F32) + zr2[2].astype(F32) + zr2[4].astype(F32)
        for c in cross_a + [back_a] + cross_b + [back_b] + cross2 + [back2]:
            c.wait_send()

    @pl.when(depth == 0)
    def _():
        back_b.wait_recv()
        put_b(b_buf[0].astype(F32) + zr_b[5].astype(F32))
        back2.wait_recv()
        att_sum[...] = att_buf[0].astype(F32) + zr2[5].astype(F32)
        for c in ends_a + ends_b + ends2:
            c.wait_send()

    for c in scatter1 + spread + scatter2 + x_b + [x_a] + x_att:
        c.wait_send()


def split_kernel(in_grad, mlp_sum, att_sum, in_grad_out, value_rows, out_rows_t, up_rows, down_rows_t):
    local, ff = value_rows.shape[1], up_rows.shape[1]
    in_grad_out[...] = in_grad[...]
    down_rows_t[...] = mlp_sum[:, 0:ff]
    up_rows[...] = mlp_sum[:, ff:2 * ff]
    out_rows_t[...] = att_sum[:, 0:local]
    value_rows[...] = att_sum[:, local:2 * local]


def on_device_fused(inputs, middle, out_grad, cached_maps, w_value, w_out, w_up, w_down):
    tok, width = inputs.shape
    local, ff = w_value.shape[1], w_up.shape[1]
    heads_here = cached_maps.shape[1]
    piece = width // lax.axis_size("img")
    share = tok // 4
    late = ff - EARLY
    vmem = pl.BlockSpec(memory_space=pltpu.VMEM)
    shape = jax.ShapeDtypeStruct
    sums = pl.pallas_call(
        block_kernel,
        out_shape=(
            shape((share, width), BF16),
            shape((piece, 2 * ff), F32),
            shape((piece, 2 * local), F32),
        ),
        in_specs=[pl.BlockSpec(memory_space=pl.ANY)] * 8,
        out_specs=(vmem,) * 3,
        scratch_shapes=[
            pltpu.VMEM((tok, width), BF16),
            pltpu.VMEM((tok, width), BF16),
            pltpu.VMEM((tok, width), BF16),
            pltpu.VMEM((heads_here, tok, tok), BF16),
            pltpu.VMEM((local, width), BF16),
            pltpu.VMEM((local, width), BF16),
            pltpu.VMEM((width, ff), BF16),
            pltpu.VMEM((ff, width), BF16),
            pltpu.VMEM((width, tok), BF16),
            pltpu.VMEM((width, tok), BF16),
            pltpu.VMEM((width, tok), BF16),
            pltpu.VMEM((width, tok), BF16),
            pltpu.VMEM((tok, ff), BF16),
            pltpu.VMEM((tok, ff), BF16),
            pltpu.VMEM((tok, local), BF16),
            pltpu.VMEM((tok, local), BF16),
            pltpu.VMEM((2, tok, width), BF16),
            pltpu.VMEM((3, share, width), BF16),
            pltpu.VMEM((3, share, width), BF16),
            pltpu.VMEM((tok, width), BF16),
            pltpu.VMEM((share, width), F32),
            pltpu.VMEM((4, 2 * piece, 2 * EARLY), BF16),
            pltpu.VMEM((8, piece, 2 * late), BF16),
            pltpu.VMEM((8, piece, 2 * local), BF16),
            pltpu.VMEM((piece, 2 * EARLY), BF16),
            pltpu.VMEM((4, piece, 2 * late), BF16),
            pltpu.VMEM((4, piece, 2 * local), BF16),
            pltpu.VMEM((6, 2 * piece, 2 * EARLY), BF16),
            pltpu.VMEM((3, 2 * piece, 2 * EARLY), BF16),
            pltpu.VMEM((6, piece, 2 * late), BF16),
            pltpu.VMEM((3, piece, 2 * late), BF16),
            pltpu.VMEM((6, piece, 2 * local), BF16),
            pltpu.VMEM((3, piece, 2 * local), BF16),
            pltpu.VMEM((2, piece, 2 * EARLY), BF16),
            pltpu.SemaphoreType.DMA((8,)),
            pltpu.SemaphoreType.DMA((36,)),
            pltpu.SemaphoreType.DMA((36,)),
        ],
        compiler_params=pltpu.CompilerParams(
            collective_id=0, has_side_effects=True, vmem_limit_bytes=56 * 1024 * 1024
        ),
    )(inputs, middle, out_grad, cached_maps[0], w_value.T, w_out, w_up, w_down)
    in_grad, value_rows, out_rows_t, up_rows, down_rows_t = pl.pallas_call(
        split_kernel,
        out_shape=(
            shape((share, width), BF16),
            shape((piece, local), F32),
            shape((piece, local), F32),
            shape((piece, ff), F32),
            shape((piece, ff), F32),
        ),
        in_specs=[vmem] * 3,
        out_specs=(vmem,) * 5,
    )(*sums)
    return in_grad, value_rows, out_rows_t.T, up_rows, down_rows_t.T


def solution(mesh):
    fused = mesh.shape["img"] == 8 and mesh.shape["head"] == 4
    return jax.shard_map(
        on_device_fused if fused else on_device,
        mesh=mesh,
        in_specs=(
            P("img", None),
            P("img", None),
            P("img", None),
            P("img", "head", None, None),
            P(None, "head"),
            P("head", None),
            P(None, "head"),
            P("head", None),
        ),
        out_specs=(
            P(("img", "head"), None),
            P("img", "head"),
            P("head", "img"),
            P("img", "head"),
            P("head", "img"),
        ),
        check_vma=False,
    )
```

```python
import jax
import jax.numpy as jnp
from jax import lax
from jax.experimental import pallas as pl
from jax.experimental.pallas import tpu as pltpu
from jax.sharding import PartitionSpec as P


def norm_rows(rows):
    centre = rows - jnp.mean(rows, axis=-1, keepdims=True)
    spread = jnp.mean(centre * centre, axis=-1, keepdims=True)
    return centre * lax.rsqrt(spread + 1e-06)


def norm_back(rows, grad):
    centre = rows - jnp.mean(rows, axis=-1, keepdims=True)
    factor = lax.rsqrt(jnp.mean(centre * centre, axis=-1, keepdims=True) + 1e-06)
    normed = centre * factor
    return factor * (
        grad
        - jnp.mean(grad, axis=-1, keepdims=True)
        - normed * jnp.mean(grad * normed, axis=-1, keepdims=True)
    )


def gelu_tanh(pre):
    return jax.nn.gelu(pre, approximate=True)


def on_device(inputs, middle, out_grad, cached_maps, w_value, w_out, w_up, w_down):
    tok_rows = inputs.shape[0]
    heads_here = cached_maps.shape[1]
    share = tok_rows // lax.axis_size("head")
    first = lax.axis_index("head") * share
    maps_here = cached_maps[0]
    normed_in = norm_rows(inputs.astype(jnp.float32)).astype(jnp.bfloat16)
    values = jnp.dot(normed_in, w_value, preferred_element_type=jnp.float32).astype(jnp.bfloat16)
    head_size = values.shape[1] // heads_here
    attended = jnp.einsum(
        "htk,khd->thd",
        maps_here,
        values.reshape(tok_rows, heads_here, head_size),
        preferred_element_type=jnp.float32,
    )
    attended = attended.astype(jnp.bfloat16).reshape(tok_rows, -1)
    middle_f = middle.astype(jnp.float32)
    normed_mid = norm_rows(middle_f).astype(jnp.bfloat16)
    pre = jnp.dot(normed_mid, w_up, preferred_element_type=jnp.float32)
    hidden = gelu_tanh(pre).astype(jnp.bfloat16)
    hidden_grad = jnp.einsum("td,fd->tf", out_grad, w_down, preferred_element_type=jnp.float32)
    pre_grad = jax.vjp(gelu_tanh, pre)[1](hidden_grad)[0].astype(jnp.bfloat16)
    down_term = jnp.einsum("tf,td->fd", hidden, out_grad, preferred_element_type=jnp.float32)
    mid_part = jnp.einsum("tf,df->td", pre_grad, w_up, preferred_element_type=jnp.float32)
    out_rows = lax.dynamic_slice_in_dim(out_grad, first, share, 0).astype(jnp.float32)
    mid_share = lax.psum_scatter(mid_part, "head", scatter_dimension=0, tiled=True)
    mid_own = out_rows + norm_back(lax.dynamic_slice_in_dim(middle_f, first, share, 0), mid_share)
    mid_grad_b = lax.all_gather(mid_own.astype(jnp.bfloat16), "head", axis=0, tiled=True)
    outproj_term = jnp.einsum("te,td->ed", attended, mid_grad_b, preferred_element_type=jnp.float32)
    att_grad = jnp.einsum(
        "td,ed->te", mid_grad_b, w_out, preferred_element_type=jnp.float32
    ).astype(jnp.bfloat16)
    value_grad = jnp.einsum(
        "htk,thd->khd",
        maps_here,
        att_grad.reshape(tok_rows, heads_here, head_size),
        preferred_element_type=jnp.float32,
    )
    value_grad = value_grad.astype(jnp.bfloat16).reshape(tok_rows, -1)
    input_part = jnp.einsum("te,de->td", value_grad, w_value, preferred_element_type=jnp.float32)
    inputs_own = lax.dynamic_slice_in_dim(inputs, first, share, 0).astype(jnp.float32)
    input_share = lax.psum_scatter(input_part, "head", scatter_dimension=0, tiled=True)
    in_grad = (mid_own + norm_back(inputs_own, input_share)).astype(jnp.bfloat16)
    picked = normed_mid
    up_term = jnp.einsum("tr,tf->rf", picked, pre_grad, preferred_element_type=jnp.float32)
    picked = normed_in
    value_term = jnp.einsum("tr,te->re", picked, value_grad, preferred_element_type=jnp.float32)
    grad_down, grad_out = (
        lax.psum_scatter(down_term, "img", scatter_dimension=1, tiled=True),
        lax.psum_scatter(outproj_term, "img", scatter_dimension=1, tiled=True),
    )
    grad_up, grad_value = (
        lax.psum_scatter(up_term, "img", scatter_dimension=0, tiled=True),
        lax.psum_scatter(value_term, "img", scatter_dimension=0, tiled=True),
    )
    return (in_grad, grad_value, grad_out, grad_up, grad_down)


MESH = pl.DeviceIdType.MESH
F32 = jnp.float32
BF16 = jnp.bfloat16
EARLY = 128
GELU_C = 0.7978845608028654


def dot_nn(a, b):
    return lax.dot_general(a, b, (((1,), (0,)), ((), ())), preferred_element_type=F32)


def dot_nt(a, b):
    return lax.dot_general(a, b, (((1,), (1,)), ((), ())), preferred_element_type=F32)


def dot_tn(a, b):
    return lax.dot_general(a, b, (((0,), (0,)), ((), ())), preferred_element_type=F32)


def gelu_and_slope(pre):
    square = pre * pre
    tanh = jnp.tanh(GELU_C * pre * (1.0 + 0.044715 * square))
    half = 0.5 * (1.0 + tanh)
    slope = half + 0.5 * pre * (1.0 - tanh * tanh) * (GELU_C * (1.0 + 3 * 0.044715 * square))
    return pre * half, slope


def block_kernel(
    inputs_h, middle_h, out_grad_h, maps_h, w_value_h, w_out_h, w_up_h, w_down_h,
    in_grad, mlp_sum, att_sum,
    inputs, middle, out_grad, maps, w_value_t, w_out, w_up, w_down,
    nmt, ogt, nint, midbt, hid, prg, attd, vgr, mp, rs1, rs2, midb, mid_own,
    a_buf, b_buf, att_buf, xr_a, xr_b, xr, zr_a, zs_a, zr_b, zs_b, zr2, zs2, xs_a,
    local_sem, send_sem, recv_sem,
):
    tok, width = inputs.shape
    share = tok // 4
    heads_here = maps.shape[0]
    local = attd.shape[1]
    hdim = local // heads_here
    ff = hid.shape[1]
    early = a_buf.shape[2] // 2
    late = ff - early
    piece = mlp_sum.shape[0]
    img = lax.axis_index("img")
    head = lax.axis_index("head")
    z = img // 2
    x = img % 2
    upper = z // 2
    depth = z % 2 * (1 - 2 * upper) + upper
    x_peer = {"img": z * 2 + (1 - x)}
    side_peer = {"img": (z + 1 - 2 * (z % 2)) * 2 + x}
    across_peer = {"img": (3 - z) * 2 + x}
    head_ids = [(head + p) % 4 for p in (1, 2, 3)]

    def copy(src, dst, sem, peer):
        return pltpu.make_async_remote_copy(
            src_ref=src, dst_ref=dst, send_sem=send_sem.at[sem], recv_sem=recv_sem.at[sem],
            device_id=peer, device_id_type=MESH,
        )

    barrier = pltpu.get_barrier_semaphore()
    for peer in [x_peer, side_peer, across_peer] + [{"head": h} for h in head_ids]:
        pl.semaphore_signal(barrier, inc=1, device_id=peer, device_id_type=MESH)
    loads = [
        pltpu.make_async_copy(src, dst, local_sem.at[i])
        for i, (src, dst) in enumerate([
            (middle_h, middle), (w_up_h, w_up), (out_grad_h, out_grad), (w_down_h, w_down),
            (inputs_h, inputs), (w_value_h, w_value_t), (maps_h, maps), (w_out_h, w_out),
        ])
    ]
    for c in loads:
        c.start()
    loads[0].wait()
    normed = norm_rows(middle[...].astype(F32)).astype(BF16)
    nmt[...] = normed.T
    loads[2].wait()
    ogt[...] = out_grad[...].T
    loads[1].wait()
    pre = dot_nn(normed, w_up[...])
    value, slope = gelu_and_slope(pre)
    hid[...] = value.astype(BF16)
    loads[3].wait()
    prg[...] = (slope * dot_nt(out_grad[...], w_down[...])).astype(BF16)

    def scatter(slot, landing, first_sem):
        return [
            copy(mp.at[slot, pl.ds(pl.multiple_of(h * share, share), share)], landing.at[p], first_sem + p, {"head": h})
            for p, h in enumerate(head_ids)
        ]

    own = pl.ds(pl.multiple_of(head * share, share), share)

    def actual(c):
        return c * (1 - 2 * upper) + 3 * upper

    def chunk(c, at_x):
        return pl.ds(pl.multiple_of((actual(c) * 2 + at_x) * piece, piece), piece)

    def exchange(buf, zr, zs, first_sem):
        ends = [copy(buf.at[c], zr.at[i], first_sem + i, side_peer) for i, c in enumerate((3, 2, 1))]
        cross = [copy(zs.at[i], zr.at[3 + i], first_sem + 3 + i, across_peer) for i in range(2)]
        back = copy(zs.at[2], zr.at[5], first_sem + 5, side_peer)
        return ends, cross, back

    ends_a, cross_a, back_a = exchange(a_buf, zr_a, zs_a, 18)
    ends_b, cross_b, back_b = exchange(b_buf, zr_b, zs_b, 24)
    ends2, cross2, back2 = exchange(att_buf, zr2, zs2, 30)

    def at_end(start):
        @pl.when(depth == 0)
        def _():
            start()

    def add(buf, zs, zr, slot, c, i):
        zs[slot] = (buf[c].astype(F32) + zr[i].astype(F32)).astype(BF16)

    pl.semaphore_wait(barrier, 6)
    order = (3, 2, 1 - depth, depth)
    x_b = []
    for i, c in enumerate(order):
        rows = chunk(c, 1 - x)
        b_buf[4 + c, :, 0:late] = dot_nn(ogt[rows], hid[:, early:ff]).astype(BF16)
        b_buf[4 + c, :, late:2 * late] = dot_nn(nmt[rows], prg[:, early:ff]).astype(BF16)
        x_b.append(copy(b_buf.at[4 + c], xr_b.at[i], 9 + i, x_peer))
        x_b[i].start()
        c = 3 - i
        rows = pl.ds(pl.multiple_of(actual(c) * 2 * piece, piece), 2 * piece)
        a_buf[c, :, 0:early] = dot_nn(ogt[rows], hid[:, 0:early]).astype(BF16)
        a_buf[c, :, early:2 * early] = dot_nn(nmt[rows], prg[:, 0:early]).astype(BF16)
        if i < 3:
            at_end(ends_a[i].start)
        if i == 0:
            mp[0] = dot_nt(prg[...], w_up[...]).astype(BF16)
            scatter1 = scatter(0, rs1, 0)
            for k in scatter1:
                k.start()
    for c in (3, 2, 1, 0):
        rows = chunk(c, x)
        b_buf[c, :, 0:late] = dot_nn(ogt[rows], hid[:, early:ff]).astype(BF16)
        b_buf[c, :, late:2 * late] = dot_nn(nmt[rows], prg[:, early:ff]).astype(BF16)

    for c in loads[4:]:
        c.wait()
    normed_in = norm_rows(inputs[...].astype(F32)).astype(BF16)
    nint[...] = normed_in.T
    values = dot_nt(normed_in, w_value_t[...]).astype(BF16)
    column = lax.broadcasted_iota(jnp.int32, (tok, local), 1)

    def own_columns(array, h):
        keep = (column >= h * hdim) & (column < (h + 1) * hdim)
        return jnp.where(keep, array, jnp.zeros_like(array))

    total = dot_nn(maps[0], own_columns(values, 0))
    for h in range(1, heads_here):
        total = total + dot_nn(maps[h], own_columns(values, h))
    attd[...] = total.astype(BF16)

    def pass_on(buf, zr, zs, ends, cross, i):
        ends[i].wait_recv()
        add(buf, zs, zr, i, 3 - i, i)
        cross[i].start()

    def give_back(buf, zr, zs, cross, back):
        cross[0].wait_recv()
        add(buf, zs, zr, 2, 0, 3)
        back.start()

    @pl.when(depth == 1)
    def _():
        pass_on(a_buf, zr_a, zs_a, ends_a, cross_a, 0)

    for c in scatter1:
        c.wait_recv()
    grad_sum = mp[0, own].astype(F32) + rs1[0].astype(F32) + rs1[1].astype(F32) + rs1[2].astype(F32)
    mid_rows = out_grad[own].astype(F32) + norm_back(middle[own].astype(F32), grad_sum)
    mid_own[...] = mid_rows
    midb[own] = mid_rows.astype(BF16)
    spread = [copy(midb.at[own], midb.at[own], 3 + p, {"head": h}) for p, h in enumerate(head_ids)]
    for c in spread:
        c.start()

    def settle_b(i):
        c = order[i]
        x_b[i].wait_recv()
        b_buf[c] = (b_buf[c].astype(F32) + xr_b[i].astype(F32)).astype(BF16)
        if i < 3:
            at_end(ends_b[i].start)

    settle_b(0)

    @pl.when(depth == 1)
    def _():
        pass_on(a_buf, zr_a, zs_a, ends_a, cross_a, 1)
        give_back(a_buf, zr_a, zs_a, cross_a, back_a)

    x_a = copy(xs_a.at[1 - x], xr_a, 13, x_peer)

    def split_a(total):
        xs_a[0] = total[0:piece].astype(BF16)
        xs_a[1] = total[piece:2 * piece].astype(BF16)

    @pl.when(depth == 1)
    def _():
        ends_a[2].wait_recv()
        cross_a[1].wait_recv()
        split_a(a_buf[1].astype(F32) + zr_a[2].astype(F32) + zr_a[4].astype(F32))
        x_a.start()

    @pl.when(depth == 0)
    def _():
        back_a.wait_recv()
        split_a(a_buf[0].astype(F32) + zr_a[5].astype(F32))
        x_a.start()

    settle_b(1)

    @pl.when(depth == 1)
    def _():
        pass_on(b_buf, zr_b, zs_b, ends_b, cross_b, 0)

    for c in spread:
        c.wait_recv()
    att_grad = dot_nt(midb[...], w_out[...]).astype(BF16)
    total = dot_tn(maps[0], own_columns(att_grad, 0))
    for h in range(1, heads_here):
        total = total + dot_tn(maps[h], own_columns(att_grad, h))
    vgr[...] = total.astype(BF16)
    midbt[...] = midb[...].T

    x_att = []
    for i, c in enumerate(order):
        rows = chunk(c, 1 - x)
        att_buf[4 + c, :, 0:local] = dot_nn(midbt[rows], attd[...]).astype(BF16)
        att_buf[4 + c, :, local:2 * local] = dot_nn(nint[rows], vgr[...]).astype(BF16)
        x_att.append(copy(att_buf.at[4 + c], xr.at[i], 14 + i, x_peer))
        x_att[i].start()
    mp[1] = dot_nn(vgr[...], w_value_t[...]).astype(BF16)
    scatter2 = scatter(1, rs2, 6)
    for c in scatter2:
        c.start()
    settle_b(2)

    @pl.when(depth == 1)
    def _():
        pass_on(b_buf, zr_b, zs_b, ends_b, cross_b, 1)
        give_back(b_buf, zr_b, zs_b, cross_b, back_b)

    for c in (3, 2, 1, 0):
        rows = chunk(c, x)
        att_buf[c, :, 0:local] = dot_nn(midbt[rows], attd[...]).astype(BF16)
        att_buf[c, :, local:2 * local] = dot_nn(nint[rows], vgr[...]).astype(BF16)

    settle_b(3)

    def settle_att(i):
        c = order[i]
        x_att[i].wait_recv()
        att_buf[c] = (att_buf[c].astype(F32) + xr[i].astype(F32)).astype(BF16)
        if i < 3:
            at_end(ends2[i].start)

    settle_att(0)
    for c in scatter2:
        c.wait_recv()
    grad_sum = mp[1, own].astype(F32) + rs2[0].astype(F32) + rs2[1].astype(F32) + rs2[2].astype(F32)
    in_grad[...] = (mid_own[...] + norm_back(inputs[own].astype(F32), grad_sum)).astype(BF16)
    x_a.wait_recv()
    total = xs_a[x].astype(F32) + xr_a[...].astype(F32)
    mlp_sum[:, 0:early] = total[:, 0:early]
    mlp_sum[:, ff:ff + early] = total[:, early:2 * early]
    settle_att(1)

    @pl.when(depth == 1)
    def _():
        pass_on(att_buf, zr2, zs2, ends2, cross2, 0)

    settle_att(2)

    @pl.when(depth == 1)
    def _():
        pass_on(att_buf, zr2, zs2, ends2, cross2, 1)
        give_back(att_buf, zr2, zs2, cross2, back2)

    settle_att(3)

    def put_b(total):
        mlp_sum[:, early:ff] = total[:, 0:late]
        mlp_sum[:, ff + early:2 * ff] = total[:, late:2 * late]

    @pl.when(depth == 1)
    def _():
        ends_b[2].wait_recv()
        cross_b[1].wait_recv()
        put_b(b_buf[1].astype(F32) + zr_b[2].astype(F32) + zr_b[4].astype(F32))
        ends2[2].wait_recv()
        cross2[1].wait_recv()
        att_sum[...] = att_buf[1].astype(F32) + zr2[2].astype(F32) + zr2[4].astype(F32)
        for c in cross_a + [back_a] + cross_b + [back_b] + cross2 + [back2]:
            c.wait_send()

    @pl.when(depth == 0)
    def _():
        back_b.wait_recv()
        put_b(b_buf[0].astype(F32) + zr_b[5].astype(F32))
        back2.wait_recv()
        att_sum[...] = att_buf[0].astype(F32) + zr2[5].astype(F32)
        for c in ends_a + ends_b + ends2:
            c.wait_send()

    for c in scatter1 + spread + scatter2 + x_b + [x_a] + x_att:
        c.wait_send()


def split_kernel(in_grad, mlp_sum, att_sum, in_grad_out, value_rows, out_rows_t, up_rows, down_rows_t):
    local, ff = value_rows.shape[1], up_rows.shape[1]
    in_grad_out[...] = in_grad[...]
    down_rows_t[...] = mlp_sum[:, 0:ff]
    up_rows[...] = mlp_sum[:, ff:2 * ff]
    out_rows_t[...] = att_sum[:, 0:local]
    value_rows[...] = att_sum[:, local:2 * local]


def on_device_fused(inputs, middle, out_grad, cached_maps, w_value, w_out, w_up, w_down):
    tok, width = inputs.shape
    local, ff = w_value.shape[1], w_up.shape[1]
    heads_here = cached_maps.shape[1]
    piece = width // lax.axis_size("img")
    share = tok // 4
    late = ff - EARLY
    vmem = pl.BlockSpec(memory_space=pltpu.VMEM)
    shape = jax.ShapeDtypeStruct
    sums = pl.pallas_call(
        block_kernel,
        out_shape=(
            shape((share, width), BF16),
            shape((piece, 2 * ff), F32),
            shape((piece, 2 * local), F32),
        ),
        in_specs=[pl.BlockSpec(memory_space=pl.ANY)] * 8,
        out_specs=(vmem,) * 3,
        scratch_shapes=[
            pltpu.VMEM((tok, width), BF16),
            pltpu.VMEM((tok, width), BF16),
            pltpu.VMEM((tok, width), BF16),
            pltpu.VMEM((heads_here, tok, tok), BF16),
            pltpu.VMEM((local, width), BF16),
            pltpu.VMEM((local, width), BF16),
            pltpu.VMEM((width, ff), BF16),
            pltpu.VMEM((ff, width), BF16),
            pltpu.VMEM((width, tok), BF16),
            pltpu.VMEM((width, tok), BF16),
            pltpu.VMEM((width, tok), BF16),
            pltpu.VMEM((width, tok), BF16),
            pltpu.VMEM((tok, ff), BF16),
            pltpu.VMEM((tok, ff), BF16),
            pltpu.VMEM((tok, local), BF16),
            pltpu.VMEM((tok, local), BF16),
            pltpu.VMEM((2, tok, width), BF16),
            pltpu.VMEM((3, share, width), BF16),
            pltpu.VMEM((3, share, width), BF16),
            pltpu.VMEM((tok, width), BF16),
            pltpu.VMEM((share, width), F32),
            pltpu.VMEM((4, 2 * piece, 2 * EARLY), BF16),
            pltpu.VMEM((8, piece, 2 * late), BF16),
            pltpu.VMEM((8, piece, 2 * local), BF16),
            pltpu.VMEM((piece, 2 * EARLY), BF16),
            pltpu.VMEM((4, piece, 2 * late), BF16),
            pltpu.VMEM((4, piece, 2 * local), BF16),
            pltpu.VMEM((6, 2 * piece, 2 * EARLY), BF16),
            pltpu.VMEM((3, 2 * piece, 2 * EARLY), BF16),
            pltpu.VMEM((6, piece, 2 * late), BF16),
            pltpu.VMEM((3, piece, 2 * late), BF16),
            pltpu.VMEM((6, piece, 2 * local), BF16),
            pltpu.VMEM((3, piece, 2 * local), BF16),
            pltpu.VMEM((2, piece, 2 * EARLY), BF16),
            pltpu.SemaphoreType.DMA((8,)),
            pltpu.SemaphoreType.DMA((36,)),
            pltpu.SemaphoreType.DMA((36,)),
        ],
        compiler_params=pltpu.CompilerParams(
            collective_id=0, has_side_effects=True, vmem_limit_bytes=56 * 1024 * 1024
        ),
    )(inputs, middle, out_grad, cached_maps[0], w_value.T, w_out, w_up, w_down)
    in_grad, value_rows, out_rows_t, up_rows, down_rows_t = pl.pallas_call(
        split_kernel,
        out_shape=(
            shape((share, width), BF16),
            shape((piece, local), F32),
            shape((piece, local), F32),
            shape((piece, ff), F32),
            shape((piece, ff), F32),
        ),
        in_specs=[vmem] * 3,
        out_specs=(vmem,) * 5,
    )(*sums)
    return in_grad, value_rows, out_rows_t.T, up_rows, down_rows_t.T


def solution(mesh):
    fused = mesh.shape["img"] == 8 and mesh.shape["head"] == 4
    return jax.shard_map(
        on_device_fused if fused else on_device,
        mesh=mesh,
        in_specs=(
            P("img", None),
            P("img", None),
            P("img", None),
            P("img", "head", None, None),
            P(None, "head"),
            P("head", None),
            P(None, "head"),
            P("head", None),
        ),
        out_specs=(
            P(("img", "head"), None),
            P("img", "head"),
            P("head", "img"),
            P("img", "head"),
            P("head", "img"),
        ),
        check_vma=False,
    )
```
